32 devices in a mesh: gz: 4 (over z), xy: 8 (over y, x, core).
Axes of the slice: x: 2, y: 2, z: 4, core: 2. Of those that a mesh axis runs over, the one named last changes fastest.
Arguments:
- features: bfloat16 [48, 16, 160, 256], P(None, 'gz', 'xy'), may hold values from -6 to 6
- first_weight: bfloat16 [3, 3, 3, 48, 48], replicated, may hold values from -0.15625 to 0.15625
- first_bias: float32 [48], replicated, may hold values from -0.5 to 0.5
- second_weight: bfloat16 [3, 3, 3, 64, 48], replicated, may hold values from -0.15625 to 0.15625
- second_bias: float32 [64], replicated, may hold values from -0.5 to 0.5
- labels: int32 [16, 160, 256], P('gz', 'xy'), may hold values from 0 to 4095, as said below
- blocks: int32 [4, 8, 256, 128], P('gz', 'xy'), may hold values from -1 to 20479, as said below
- owner_map: int32 [4096], replicated, may hold values from 0 to 4095, as said below
Outputs:
- mean_embedding: float32 [4096, 64], P(('gz', 'xy'))
- covariance: float32 [4096, 4096], P(('gz', 'xy'))
The draws below stay inside these ranges and needn't reach their ends.
Inputs may be any that keep to these rules, and one draw needn't show every extreme that they name: `labels`: all voxels listed in one block carry the same label. A tile's 256 blocks together list every voxel of the tile exactly once. A block lists a quarter of 128 to 128 voxels whose indices follow one another in ascending order, then -1 to its end. In each tile at most 24 blocks have rows owner_map[label] within one device's 128 output rows, and in every draw the rows of some devices receive exactly 24 blocks from every tile. `owner_map`: A permutation of the output rows.
All inputs are finite; a program needn't handle non-finite values.
Results may differ from the reference program's by a relative error of at most 0.0042.
Values may be sent and summed in bfloat16 or wider, within the bound.
No kernel may reach another device: no remote copies, remote signals or barrier semaphores. Data moves between devices by JAX's collectives and lax.ppermute only.
A program may use at most 128 MiB of HBM per device.

```python
import jax
import jax.numpy as jnp
from jax import lax

IN_CH = 48
MID_CH = 48
EMB_CH = 64
X_LEN = 256
Z_DEV = 4
Y_DEV = 20
SV_DEV = 128
BLOCK_LEN = 128
Z_CELLS = 16
Y_CELLS = 160
OWNERS = 32
SEG_COUNT = 640
BLOCKS_DEV = 256
SLOT_CAP = 24
HEAVY_OWNERS = 4
SUPERVOXELS = 4096
N_GZ = 4
N_XY = 8


def layout(key):
    base = jax.random.fold_in(key, 4242)
    perm_key, heavy_key, offset_key, tiles_key = jax.random.split(base, 4)
    owner_map = jax.random.permutation(perm_key, SUPERVOXELS).astype(jnp.int32)
    inverse = jnp.zeros((SUPERVOXELS,), jnp.int32).at[owner_map].set(jnp.arange(SUPERVOXELS, dtype=jnp.int32))
    shuffled = jax.random.permutation(heavy_key, OWNERS).astype(jnp.int32)
    heavy_owners = shuffled[:HEAVY_OWNERS]
    light_owners = shuffled[HEAVY_OWNERS:]
    offsets = jax.random.randint(offset_key, (OWNERS,), 0, SV_DEV, dtype=jnp.int32)
    half_cap = SLOT_CAP // 2
    pool_size = (OWNERS - HEAVY_OWNERS) * half_cap
    seg_len = BLOCK_LEN // 4

    def one_tile(tile_key):
        pick_key, order_key, local_key, length_key = jax.random.split(tile_key, 4)
        heavy_part = jnp.repeat(heavy_owners, SLOT_CAP)
        picks = jax.random.permutation(pick_key, pool_size).astype(jnp.int32)[:BLOCKS_DEV - HEAVY_OWNERS * SLOT_CAP]
        light_part = light_owners[picks // half_cap]
        block_owner = jnp.concatenate([heavy_part, light_part])
        block_owner = block_owner[jax.random.permutation(order_key, BLOCKS_DEV).astype(jnp.int32)]
        local_draw = jax.random.randint(local_key, (BLOCKS_DEV,), 0, SV_DEV, dtype=jnp.int32)
        local_rows = (local_draw * local_draw // SV_DEV * local_draw // SV_DEV + offsets[block_owner]) % SV_DEV
        block_labels = inverse[block_owner * SV_DEV + local_rows]
        first_len = jax.random.randint(length_key, (BLOCKS_DEV // 2,), 1, 5, dtype=jnp.int32)
        lengths = jnp.stack([first_len, 5 - first_len], axis=1).reshape(BLOCKS_DEV)
        starts = jnp.cumsum(lengths) - lengths
        within = jnp.arange(BLOCK_LEN, dtype=jnp.int32)
        lists = jnp.where(within[None, :] < (lengths * seg_len)[:, None], starts[:, None] * seg_len + within[None, :], -1)
        run_marks = jnp.zeros((SEG_COUNT,), jnp.int32).at[starts].set(1)
        seg_block = jnp.cumsum(run_marks) - 1
        voxel_label = jnp.broadcast_to(block_labels[seg_block][:, None], (SEG_COUNT, seg_len)).reshape(Z_DEV, Y_DEV, X_LEN)
        return (voxel_label, lists.astype(jnp.int32))
    tile_keys = jax.random.split(tiles_key, OWNERS)
    tile_labels, tile_lists = jax.vmap(one_tile)(tile_keys)
    labels = tile_labels.reshape(N_GZ, N_XY, Z_DEV, Y_DEV, X_LEN).transpose(0, 2, 1, 3, 4).reshape(N_GZ * Z_DEV, N_XY * Y_DEV, X_LEN)
    lists = tile_lists.reshape(N_GZ, N_XY, BLOCKS_DEV, BLOCK_LEN)
    return (labels.astype(jnp.int32), lists, owner_map)


def draw_labels(key, part):
    return layout(key)[0]


def draw_blocks(key, part):
    return layout(key)[1]


def draw_owner_map(key, part):
    return layout(key)[2]


def steps_of(key, extent, cuts, least, top_value):
    factor_of, own = 1.0, jax.random.fold_in(key, 6)
    for position, blocks in cuts:
        heights = jnp.exp(jax.random.uniform(jax.random.fold_in(own, position), (blocks,), jnp.float32, least / len(cuts), top_value / len(cuts)))
        factor_of = factor_of * jnp.repeat(heights, extent[position] // blocks).reshape([-1 if axis == position else 1 for axis in range(len(extent))])
    return factor_of


def centred(stream_key, extent, deviation, most, shards=(), kind=jnp.bfloat16):
    array = jax.random.normal(stream_key, extent, jnp.float32) * deviation
    if len(shards) > 0:
        array = steps_of(stream_key, extent, shards, -0.22, 0.18) * array
    return jnp.clip(array, min=-most, max=most).astype(kind)


def setup_inputs(seed: int = 0) -> dict:
    streams_of = jax.random.split(jax.random.key(seed), 9)
    features = centred(streams_of[0], (IN_CH, Z_CELLS, Y_CELLS, X_LEN), 1.0, 6.0, ((1, 4), (2, 8)))
    first_weight = centred(streams_of[1], (3, 3, 3, MID_CH, IN_CH), (27 * IN_CH) ** -0.5, 0.15625)
    first_bias = jnp.clip(jax.random.uniform(streams_of[2], (MID_CH,), jnp.float32, -0.5, 0.5), -0.5, 0.5)
    second_weight = centred(streams_of[3], (3, 3, 3, EMB_CH, MID_CH), (27 * MID_CH) ** -0.5, 0.15625)
    second_bias = jnp.clip(jax.random.uniform(streams_of[4], (EMB_CH,), jnp.float32, -0.5, 0.5), -0.5, 0.5)
    labels = draw_labels(jax.random.fold_in(streams_of[8], 71), 0)
    blocks = draw_blocks(jax.random.fold_in(streams_of[8], 71), 0)
    owner_map = draw_owner_map(jax.random.fold_in(streams_of[8], 71), 0)
    return {"features": features, "first_weight": first_weight, "first_bias": first_bias, "second_weight": second_weight, "second_bias": second_bias, "labels": labels, "blocks": blocks, "owner_map": owner_map}


CONV_LAYOUT = ("NCDHW", "DHWOI", "NCDHW")


def convolve(volume, weight, bias):
    summed = lax.conv_general_dilated(volume[None], weight, (1, 1, 1), ((1, 1), (1, 1), (1, 1)), dimension_numbers=CONV_LAYOUT, preferred_element_type=jnp.float32)[0]
    return summed + bias[:, None, None, None]


def reference(features, first_weight, first_bias, second_weight, second_bias, labels, blocks, owner_map):
    hidden = jax.nn.relu(convolve(features, first_weight, first_bias)).astype(jnp.bfloat16)
    embedding = convolve(hidden, second_weight, second_bias).astype(jnp.bfloat16)
    tile_lists = blocks.reshape(N_GZ * N_XY, BLOCKS_DEV, BLOCK_LEN)

    def tile_step(totals, tile):
        depth = tile // N_XY
        plane = tile % N_XY
        anchor = jnp.zeros((), jnp.int32)
        piece = lax.dynamic_slice(embedding, (anchor, (depth * Z_DEV).astype(jnp.int32), (plane * Y_DEV).astype(jnp.int32), anchor), (EMB_CH, Z_DEV, Y_DEV, X_LEN)).reshape(EMB_CH, -1)
        tile_labels = lax.dynamic_slice(labels, ((depth * Z_DEV).astype(jnp.int32), (plane * Y_DEV).astype(jnp.int32), anchor), (Z_DEV, Y_DEV, X_LEN)).reshape(-1)
        voxel_lists = tile_lists[tile]
        in_block = voxel_lists >= 0
        picked = jnp.take(piece, jnp.where(in_block, voxel_lists, 0).reshape(-1), axis=1).reshape(EMB_CH, BLOCKS_DEV, BLOCK_LEN)
        picked = jnp.where(in_block[None], picked.astype(jnp.float32), jnp.zeros((), jnp.float32))
        block_sizes = jnp.sum(in_block.astype(jnp.float32), axis=1)
        block_sums = jnp.sum(picked, axis=2).T
        block_second = jnp.einsum("cnk,dnk->ncd", picked, picked).reshape(BLOCKS_DEV, EMB_CH * EMB_CH)
        owner_rows = owner_map[tile_labels[voxel_lists[:, 0]]]
        counts, sums, second = totals
        return (counts.at[owner_rows].add(block_sizes), sums.at[owner_rows].add(block_sums), second.at[owner_rows].add(block_second)), None

    start = (jnp.zeros((SUPERVOXELS,), jnp.float32), jnp.zeros((SUPERVOXELS, EMB_CH), jnp.float32), jnp.zeros((SUPERVOXELS, EMB_CH * EMB_CH), jnp.float32))
    totals = lax.scan(tile_step, start, jnp.arange(N_GZ * N_XY, dtype=jnp.int32))[0]
    counts, sums, second = totals
    denominator = jnp.maximum(counts, 1.0)
    mean_embedding = sums / denominator[:, None]
    covariance = second / denominator[:, None] - (mean_embedding[:, :, None] * mean_embedding[:, None, :]).reshape(SUPERVOXELS, EMB_CH * EMB_CH)
    return mean_embedding, covariance
```

```python
import functools

import jax
import jax.numpy as jnp
from jax import lax
from jax.experimental import pallas as pl
from jax.experimental.pallas import tpu as pltpu
from jax.sharding import PartitionSpec as P

BF16 = jnp.bfloat16
F32 = jnp.float32
EMPTY = -200.0
ROW_LANE = 65


def dot_nn(a, b):
    return lax.dot_general(a, b, (((1,), (0,)), ((), ())), preferred_element_type=F32)


def dot_nt(a, b):
    return lax.dot_general(a, b, (((1,), (1,)), ((), ())), preferred_element_type=F32)


def regroup_kernel(x_ref, o_ref, tmp_ref):
    channels, _, rows, length = x_ref.shape
    for c in range(channels):
        value = x_ref[c, 0].astype(F32)
        for half in range(length // 128):
            part = value[:, half * 128:(half + 1) * 128]
            tmp_ref[half, pl.ds(c, rows, stride=channels), :] = part
    for half in range(length // 128):
        o_ref[0, :, half * 128:(half + 1) * 128] = tmp_ref[half].astype(BF16)


def regroup(features):
    channels, depth, rows, length = features.shape
    return pl.pallas_call(
        regroup_kernel,
        grid=(depth,),
        out_shape=jax.ShapeDtypeStruct((depth, rows * channels, length), BF16),
        in_specs=[pl.BlockSpec((channels, 1, rows, length), lambda z: (0, z, 0, 0))],
        out_specs=pl.BlockSpec((1, rows * channels, length), lambda z: (z, 0, 0)),
        scratch_shapes=[pltpu.VMEM((length // 128, rows * channels, 128), F32)],
        compiler_params=pltpu.CompilerParams(vmem_limit_bytes=48 << 20),
    )(features)


def shift_sum(raw, out):
    left, mid, right = raw[:out], raw[out:2 * out], raw[2 * out:]
    length = raw.shape[1]
    lane = lax.broadcasted_iota(jnp.int32, (out, length), 1)
    left = jnp.where(lane == 0, 0.0, pltpu.roll(left, 1, 1))
    right = jnp.where(lane == length - 1, 0.0, pltpu.roll(right, length - 1, 1))
    return mid + left + right


def tile_kernel(
    dims, meta_ref, inv_ref, place_ref, centre, below, above, before, after, c00, c01, c10, c11,
    w1_ref, w2_ref, b1_ref, b2_ref, out_ref,
    feat, hid, emb, moments, extras, sems,
):
    depth, rows, cin, mid, ech, length, devices, slots, blocks = dims
    wide, tall = rows + 4, depth + 4
    lo, hi = 2 * cin, (rows + 2) * cin
    end = wide * cin
    copies = [
        (centre, feat.at[2:depth + 2, lo:hi]),
        (below, feat.at[0:2, lo:hi]),
        (above, feat.at[depth + 2:tall, lo:hi]),
        (before, feat.at[2:depth + 2, 0:lo]),
        (after, feat.at[2:depth + 2, hi:end]),
        (c00, feat.at[0:2, 0:lo]),
        (c01, feat.at[0:2, hi:end]),
        (c10, feat.at[depth + 2:tall, 0:lo]),
        (c11, feat.at[depth + 2:tall, hi:end]),
    ]
    copies = [pltpu.make_async_copy(s, d, sems.at[k]) for k, (s, d) in enumerate(copies)]
    for copy in copies:
        copy.start()

    aug = emb.shape[1]
    tail = jnp.where(lax.broadcasted_iota(jnp.int32, (aug - ech, 128), 0) == 0, 1.0, 0.0).astype(BF16)

    @pl.loop(0, emb.shape[0])
    def _(w):
        emb[w, ech:aug, :] = tail

    emb[emb.shape[0] - 1, 0:ech, :] = jnp.zeros((ech, 128), BF16)

    @pl.loop(0, moments.shape[0] // 64)
    def _(k):
        moments[pl.ds(k * 64, 64), :] = jnp.zeros((64, 128), F32)

    empty = jnp.where(lax.broadcasted_iota(jnp.int32, (8, 128), 1) == ROW_LANE, EMPTY, 0.0)

    @pl.loop(0, extras.shape[0] // 8)
    def _(k):
        extras[pl.ds(k * 8, 8), :] = empty

    for copy in copies:
        copy.wait()

    g, j = place_ref[0], place_ref[1]
    last_g, last_j = place_ref[2], place_ref[3]
    hrows = rows + 2
    for hz in range(depth + 2):
        dead_z = False
        if hz == 0:
            dead_z = g == 0
        if hz == depth + 1:
            dead_z = g == last_g

        @pl.loop(0, hrows, unroll=2)
        def _(hy):
            at = pl.multiple_of(hy * cin, 16)
            slab = jnp.concatenate([feat[hz + k, pl.ds(at, 3 * cin), :] for k in range(3)], axis=0)
            value = shift_sum(dot_nn(w1_ref[...], slab), mid) + b1_ref[...]
            value = jnp.maximum(value, 0.0)
            dead = ((hy == 0) & (j == 0)) | ((hy == hrows - 1) & (j == last_j)) | dead_z
            value = value * jnp.where(dead, 0.0, 1.0)
            hid[hz, pl.ds(pl.multiple_of(hy * mid, 16), mid), :] = value.astype(BF16)

    for z in range(depth):

        @pl.loop(0, rows, unroll=2)
        def _(y):
            at = pl.multiple_of(y * mid, 16)
            slab = jnp.concatenate([hid[z + k, pl.ds(at, 3 * mid), :] for k in range(3)], axis=0)
            value = (shift_sum(dot_nn(w2_ref[...], slab), ech) + b2_ref[...]).astype(BF16)
            parts = length // 128
            for p in range(parts):
                emb[(z * rows + y) * parts + p, 0:ech, :] = value[:, p * 128:(p + 1) * 128]

    half = ech // 2
    lane = lax.broadcasted_iota(jnp.int32, (half, 128), 1)
    sub = lax.broadcasted_iota(jnp.int32, (half, 128), 0)
    lane16 = lax.broadcasted_iota(jnp.int32, (half // 2, 128), 1)
    lane1 = lax.broadcasted_iota(jnp.int32, (1, 128), 1)
    wlane = lax.broadcasted_iota(jnp.int32, (aug, 256), 1)

    @pl.loop(0, blocks, unroll=4)
    def _(b):
        start, count = meta_ref[0, b], meta_ref[1, b]
        slot, place, row = meta_ref[2, b], meta_ref[3, b], meta_ref[4, b]
        window = lax.shift_right_logical(start, 7)
        first = start & 127
        both = jnp.concatenate([emb[window], emb[window + 1]], axis=1)
        inside = (wlane >= first) & (wlane < first + count)
        masked = jnp.where(inside, both, jnp.zeros_like(both))
        padded = jnp.concatenate([both, jnp.zeros((128 - aug, 256), BF16)], axis=0)
        second = dot_nt(masked, padded)
        sums = second[ech:ech + 1, :]
        centred = second[0:ech, :] - second[0:ech, ech:ech + 1] * (sums * inv_ref[b])
        top, bottom = centred[0:half], centred[half:ech]
        folded = jnp.where((lane < half) & (lane < sub), pltpu.roll(bottom, 128 - half, 1), top)
        tile = jnp.where(lane16 < ech, folded[0:half // 2], pltpu.roll(folded[half // 2:], ech, 1))
        diag = jnp.sum(jnp.where(lane == sub + half, bottom, 0.0), axis=0, keepdims=True)
        extra = jnp.where(lane1 <= ech, sums, pltpu.roll(diag, ech, 1))
        extra = jnp.where(lane1 == ROW_LANE, row.astype(F32), extra)
        moments[pl.ds(place, 8, stride=slots), :] = tile[0:8]
        moments[pl.ds(place + 8 * slots, 8, stride=slots), :] = tile[8:16]
        extras[pl.ds(slot, 1), :] = extra

    @pl.loop(0, devices)
    def _(d):
        body = moments[pl.ds(pl.multiple_of(d * 16 * slots, 8), 16 * slots), :]
        out_ref[d, 0:16 * slots, :] = body.astype(BF16)
        extra = extras[pl.ds(pl.multiple_of(d * slots, 8), slots), :]
        high = extra.astype(BF16).astype(F32)
        both = jnp.concatenate([high, extra - high], axis=0)
        out_ref[d, 16 * slots:18 * slots, :] = both.astype(BF16)


def rows_kernel(dims, y_ref, mean_ref, cov_ref, extras, doubled, folded):
    devices, slots, sv, ech = dims
    half = ech // 2
    total = devices * slots
    row_of = lax.broadcasted_iota(jnp.int32, (2 * slots, 128), 0)
    col_of = lax.broadcasted_iota(jnp.int32, (2 * slots, 128), 1)
    step = jnp.where((row_of >= slots) & (col_of == ROW_LANE), float(sv), 0.0)

    @pl.loop(0, devices)
    def _(d):
        both = y_ref[d, 16 * slots:18 * slots, :].astype(F32)
        extra = both[0:slots] + both[slots:2 * slots]
        extras[pl.ds(pl.multiple_of(d * slots, 8), slots), :] = extra
        twice = jnp.concatenate([extra, extra], axis=0) + step
        doubled[pl.ds(pl.multiple_of(d * 2 * slots, 16), 2 * slots), :] = twice.astype(BF16)

    extra = extras[...]
    high = extra.astype(BF16)
    low = (extra - high.astype(F32)).astype(BF16)
    pick = jnp.where(lax.broadcasted_iota(jnp.int32, (8, 128), 1) == ROW_LANE, 1.0, 0.0).astype(BF16)
    row_line = dot_nt(pick, high)[0:1]
    hits = jnp.where(
        lax.broadcasted_iota(jnp.int32, (sv, total), 0).astype(F32) == row_line, 1.0, 0.0
    ).astype(BF16)
    totals = dot_nn(hits, high) + dot_nn(hits, low)
    count = totals[:, ech:ech + 1]
    inverse = 1.0 / jnp.maximum(count, 1.0)
    mean = totals * inverse
    mean_ref[...] = mean[:, 0:ech]

    lane_all = lax.broadcasted_iota(jnp.int32, (total, 128), 1)
    hits_t = jnp.where(lane_all.astype(F32) == extra[:, ROW_LANE:ROW_LANE + 1], 1.0, 0.0).astype(BF16)
    mean_a = mean.astype(BF16)
    rest = mean - mean_a.astype(F32)
    mean_b = rest.astype(BF16)
    mean_c = (rest - mean_b.astype(F32)).astype(BF16)
    own_mean = dot_nn(hits_t, mean_a) + dot_nn(hits_t, mean_b) + dot_nn(hits_t, mean_c)
    size = extra[:, ech:ech + 1]
    inv_size = jnp.where(size > 0.0, 1.0 / jnp.maximum(size, 1.0), 0.0)
    delta = jnp.where((lane_all < ech) & (size > 0.0), extra * inv_size - own_mean, 0.0)
    delta = delta + pltpu.roll(delta, ech, 1)
    weighted = (delta * size).astype(BF16)
    delta = delta.astype(BF16)
    eye = jnp.where(
        lax.broadcasted_iota(jnp.int32, (ech, 128), 0) == lax.broadcasted_iota(jnp.int32, (ech, 128), 1),
        1.0, 0.0,
    ).astype(BF16)
    lines = dot_nt(eye, weighted)

    pick_line = dot_nt(pick, doubled[...])[0:1]
    hits2 = jnp.where(
        lax.broadcasted_iota(jnp.int32, (2 * sv, 2 * total), 0).astype(F32) == pick_line, 1.0, 0.0
    ).astype(BF16)
    for p in range(half // 4):
        block = y_ref[:, p * 2 * slots:(p + 1) * 2 * slots, :].reshape(2 * total, 128)
        pair = dot_nn(hits2, block)
        for q in range(2):
            a = 2 * p + q
            turned = pair[q * sv:(q + 1) * sv].T
            folded[a * ech:(a + 1) * ech, :] = turned[0:ech]
            folded[(a + half // 2) * ech:(a + half // 2 + 1) * ech, :] = turned[ech:2 * ech]

    diag = totals.T[128 - half:128, :]
    sub8 = lax.broadcasted_iota(jnp.int32, (8, 128), 0)
    lane_sv = lax.broadcasted_iota(jnp.int32, (sv, 128), 1)

    def group(i, jg):
        j0 = jg * 8
        if i < half:
            ahead = folded[i * ech + j0:i * ech + j0 + 8, :]
            if j0 >= i:
                return ahead
            across = folded[pl.ds(j0 * ech + i, 8, stride=ech), :]
            if j0 + 7 < i:
                return across
            return jnp.where(sub8 + j0 >= i, ahead, across)
        if j0 < half:
            return folded[pl.ds(j0 * ech + i, 8, stride=ech), :]
        i2, j2 = i - half, j0 - half
        ahead = folded[i2 * ech + j2:i2 * ech + j2 + 8, :]
        if j2 + 7 < i2:
            return ahead
        across = folded[pl.ds(j2 * ech + i2, 8, stride=ech), :]
        if j2 > i2:
            return across
        mixed = jnp.where(sub8 + j2 < i2, ahead, across)
        return jnp.where(sub8 + j2 == i2, diag[i2:i2 + 1], mixed)

    for t in range(half):
        pieces = [group(2 * t + q, jg) for q in range(2) for jg in range(ech // 8)]
        within = jnp.concatenate(pieces, axis=0).T
        left = hits * lines[2 * t:2 * t + 1].astype(BF16)
        right = hits * lines[2 * t + 1:2 * t + 2].astype(BF16)
        between = jnp.where(lane_sv < ech, dot_nn(left, delta), dot_nn(right, delta))
        cov_ref[:, t * 128:(t + 1) * 128] = (within + between) * inverse


def permute(array, steps, sizes):
    axes = tuple(sizes)
    (na, nb) = (sizes[a] for a in axes)
    da, db = steps
    pairs = [
        (a * nb + b, (a + da) * nb + b + db)
        for a in range(na)
        for b in range(nb)
        if 0 <= a + da < na and 0 <= b + db < nb
    ]
    return lax.ppermute(array, axes, pairs)


def local(
    sizes, features, first_weight, first_bias, second_weight, second_bias, labels, blocks, owner_map
):
    channels, depth, rows, length = features.shape
    mid, ech = first_bias.shape[0], second_bias.shape[0]
    n_gz, n_xy = sizes["gz"], sizes["xy"]
    devices = n_gz * n_xy
    sv = owner_map.shape[0] // devices
    n_blocks, width = blocks.shape[2], blocks.shape[3]
    capacity = max(2, 3 * n_blocks // devices)
    slots = -(-capacity // 8) * 8

    grouped = regroup(features)
    edge = 2 * channels
    low_z, high_z = grouped[0:2], grouped[depth - 2:depth]
    low_y, high_y = grouped[:, 0:edge], grouped[:, rows * channels - edge:]
    below = permute(high_z, (1, 0), sizes)
    above = permute(low_z, (-1, 0), sizes)
    before = permute(high_y, (0, 1), sizes)
    after = permute(low_y, (0, -1), sizes)
    c00 = permute(high_y[depth - 2:], (1, 1), sizes)
    c01 = permute(low_y[depth - 2:], (1, -1), sizes)
    c10 = permute(high_y[0:2], (-1, 1), sizes)
    c11 = permute(low_y[0:2], (-1, -1), sizes)

    lists = blocks.reshape(n_blocks, width)
    starts = lists[:, 0]
    counts = jnp.sum((lists >= 0).astype(jnp.int32), axis=1)
    owner = owner_map[labels.reshape(-1)[starts]]
    target, row = owner // sv, owner % sv
    hits = (target[:, None] == jnp.arange(devices, dtype=jnp.int32)[None, :]).astype(jnp.int32)
    rank = jnp.sum((jnp.cumsum(hits, axis=0) - hits) * hits, axis=1)
    meta = jnp.stack([starts, counts, target * slots + rank, target * 16 * slots + rank, row])
    inv_counts = 1.0 / jnp.maximum(counts, 1).astype(F32)
    place = jnp.stack(
        [lax.axis_index("gz"), lax.axis_index("xy"), jnp.int32(n_gz - 1), jnp.int32(n_xy - 1)]
    ).astype(jnp.int32)

    w1 = first_weight.transpose(2, 3, 0, 1, 4).reshape(3 * mid, 9 * channels)
    w2 = second_weight.transpose(2, 3, 0, 1, 4).reshape(3 * ech, 9 * mid)
    b1 = jnp.broadcast_to(first_bias[:, None], (mid, length))
    b2 = jnp.broadcast_to(second_bias[:, None], (ech, length))

    smem = pl.BlockSpec(memory_space=pltpu.SMEM)
    vmem = pl.BlockSpec(memory_space=pltpu.VMEM)
    anywhere = pl.BlockSpec(memory_space=pl.ANY)
    dims = (depth, rows, channels, mid, ech, length, devices, slots, n_blocks)
    windows = depth * rows * length // 128
    packed = pl.pallas_call(
        functools.partial(tile_kernel, dims),
        out_shape=jax.ShapeDtypeStruct((devices, 18 * slots, 128), BF16),
        in_specs=[smem] * 3 + [anywhere] * 9 + [vmem] * 4,
        out_specs=vmem,
        scratch_shapes=[
            pltpu.VMEM((depth + 4, (rows + 4) * channels, length), BF16),
            pltpu.VMEM((depth + 2, (rows + 2) * mid, length), BF16),
            pltpu.VMEM((windows + 1, ech + 16, 128), BF16),
            pltpu.VMEM((devices * 16 * slots, 128), F32),
            pltpu.VMEM((devices * slots, 128), F32),
            pltpu.SemaphoreType.DMA((9,)),
        ],
        compiler_params=pltpu.CompilerParams(vmem_limit_bytes=56 << 20),
    )(meta, inv_counts, place, grouped, below, above, before, after, c00, c01, c10, c11, w1, w2, b1, b2)

    arrived = lax.all_to_all(packed, ("gz", "xy"), split_axis=0, concat_axis=0, tiled=True)

    total = devices * slots
    return pl.pallas_call(
        functools.partial(rows_kernel, (devices, slots, sv, ech)),
        out_shape=(
            jax.ShapeDtypeStruct((sv, ech), F32),
            jax.ShapeDtypeStruct((sv, ech * ech), F32),
        ),
        in_specs=[vmem],
        out_specs=(vmem, vmem),
        scratch_shapes=[
            pltpu.VMEM((total, 128), F32),
            pltpu.VMEM((2 * total, 128), BF16),
            pltpu.VMEM((ech // 2 * ech, 128), F32),
        ],
        compiler_params=pltpu.CompilerParams(vmem_limit_bytes=56 << 20),
    )(arrived)


def solution(mesh):
    sizes = {"gz": mesh.shape["gz"], "xy": mesh.shape["xy"]}
    return jax.shard_map(
        functools.partial(local, sizes),
        mesh=mesh,
        in_specs=(
            P(None, "gz", "xy", None),
            P(),
            P(),
            P(),
            P(),
            P("gz", "xy", None),
            P("gz", "xy", None, None),
            P(),
        ),
        out_specs=(P(("gz", "xy"), None), P(("gz", "xy"), None)),
        check_vma=False,
    )
```
